32 devices in a mesh: tg: 4 (over y, x), fft: 8 (over z, core).
Axes of the slice: x: 2, y: 2, z: 4, core: 2. Of those that a mesh axis runs over, the one named last changes fastest.
Arguments:
- coeffs: float32 [4, 2, 240, 2048], P(None, None, None, ('tg', 'fft')), may hold values from -6 to 6
- stick_count: int32 [32], replicated, may hold values from 16 to 64, as said below
- stick_column: int32 [2048], replicated, may hold values from 0 to 57599, as said below
- plane_owner: int32 [240], replicated, may hold values from 0 to 7, as said below
- potential: float32 [240, 57600], P('fft'), may hold values from -3 to 1
Outputs:
- applied: float32 [4, 2, 240, 2048], P(None, None, None, ('tg', 'fft'))
The draws below stay inside these ranges and needn't reach their ends.
Inputs may be any that keep to these rules, and one draw needn't show every extreme that they name: `stick_count`: each block of 64 slots holds at least 16 live sticks; max(1, 4 * 8 // 8) blocks are full in every draw. `stick_column`: all entries are distinct. `plane_owner`: no fft index owns more than 30 planes, and some own exactly 30.
All inputs are finite; a program needn't handle non-finite values.
Results may differ from the reference program's by a relative error of at most 0.000071.
Values sent between devices are 32-bit elements; how exact they have to be, the bound alone decides.
A program may use at most 256 MiB of HBM per device.

```python
import jax
import jax.numpy as jnp
from jax import lax

NX = 240
NY = 240
NZ = 240
BANDS = 4
S_MAX = 64
P_MAX = 30
SLOTS = 2048
PLANE_ROWS = 240
N_TG = 4
N_FFT = 8


def draw_stick_count(key, part):
    devices = N_TG * N_FFT
    low_key, pick_key = jax.random.split(jax.random.fold_in(key, 3))
    counts = jax.random.randint(low_key, (devices,), S_MAX // 4, S_MAX // 2 + 1)
    heavy_rows = jax.random.permutation(pick_key, devices)[:max(devices // 8, 1)]
    return counts.at[heavy_rows].set(S_MAX).astype(jnp.int32)


def draw_stick_column(key, part):
    shuffled = jax.random.permutation(jax.random.fold_in(key, 7), NX * NY)
    return shuffled[:N_TG * N_FFT * S_MAX].astype(jnp.int32)


def draw_plane_owner(key, part):
    plane_slots = (NZ + N_FFT - 1) // N_FFT
    total_slots = N_FFT * plane_slots
    dropped = total_slots - NZ
    drop_key, order_key = jax.random.split(jax.random.fold_in(key, 11))
    chosen = jax.random.permutation(drop_key, N_FFT)[:dropped]
    removed = jnp.zeros((total_slots,), jnp.int32).at[chosen * plane_slots + plane_slots - 1].set(1)
    retained = jnp.argsort(removed * total_slots + jnp.arange(total_slots, dtype=jnp.int32), stable=True)[:NZ]
    owners = (retained // plane_slots).astype(jnp.int32)
    placing = jax.random.permutation(order_key, NZ)
    return jnp.zeros((NZ,), jnp.int32).at[placing].set(owners)


def block_scale(rng, extent, shards, smallest, high):
    def one(dim, blocks):
        steps = jax.random.uniform(jax.random.fold_in(jax.random.fold_in(rng, 6), dim), (blocks,), jnp.float32, smallest / len(shards), high / len(shards))
        return jnp.repeat(jnp.exp(steps), extent[dim] // blocks).reshape((-1,) + (1,) * (len(extent) - dim - 1))

    factor_of = one(*shards[0])
    for cut in shards[1:]:
        factor_of = factor_of * one(*cut)
    return factor_of


def centred(rng, extent, width, most, cuts=(), kind=jnp.bfloat16):
    values = width * jax.random.normal(rng, extent, jnp.float32)
    if cuts:
        values = values * block_scale(rng, extent, cuts, -0.22, 0.18)
    return jnp.clip(values, -most, most).astype(kind)


def setup_inputs(seed: int = 0) -> dict:
    splits = jax.random.split(jax.random.key(seed), 6)
    coeffs = centred(splits[0], (BANDS, 2, NZ, SLOTS), 1.0, 6.0, ((3, 32),), jnp.float32)
    stick_count = draw_stick_count(jax.random.fold_in(splits[5], 71), 0)
    stick_column = draw_stick_column(jax.random.fold_in(splits[5], 71), 0)
    plane_owner = draw_plane_owner(jax.random.fold_in(splits[5], 71), 0)
    potential = jnp.clip(-3.0 + 4.0 * jax.random.uniform(splits[4], (PLANE_ROWS, NX * NY), jnp.float32) ** block_scale(splits[4], (PLANE_ROWS, NX * NY), ((0, 8),), -0.2, 0.2), -3.0, 1.0)
    return {"coeffs": coeffs, "stick_count": stick_count, "stick_column": stick_column, "plane_owner": plane_owner, "potential": potential}


def plane_rows_of(plane_owner, plane_slots):
    planes = jnp.arange(NZ, dtype=jnp.int32)
    same_owner = plane_owner[None, :] == plane_owner[:, None]
    earlier = planes[None, :] < planes[:, None]
    plane_ranks = jnp.sum((same_owner & earlier).astype(jnp.int32), axis=1)
    return plane_owner * plane_slots + plane_ranks


def reference(coeffs, stick_count, stick_column, plane_owner, potential):
    columns = NX * NY
    live_slots = (jnp.arange(S_MAX, dtype=jnp.int32)[None, :] < stick_count[:, None]).reshape(-1)
    target = jnp.where(live_slots, stick_column, columns)
    fetch_index = jnp.minimum(target, columns - 1)
    potential_grid = potential[plane_rows_of(plane_owner, P_MAX)].reshape(NZ, NX, NY)

    def one_band(coefficient):
        real_grid = jnp.zeros((NZ, columns), coefficient.dtype).at[:, target].add(coefficient[0], mode="drop")
        imag_grid = jnp.zeros((NZ, columns), coefficient.dtype).at[:, target].add(coefficient[1], mode="drop")
        spectrum = lax.complex(real_grid, imag_grid).reshape(NZ, NX, NY)
        wave_grid = jnp.fft.ifftn(spectrum, norm="ortho")
        applied = jnp.fft.fftn(wave_grid * potential_grid, norm="ortho").reshape(NZ, columns)
        picked = applied[:, fetch_index]
        return jnp.stack([jnp.where(live_slots, jnp.real(picked), 0.0), jnp.where(live_slots, jnp.imag(picked), 0.0)])

    return lax.map(one_band, coeffs)
```

```python
import functools
import math

import jax
import jax.numpy as jnp
import ml_dtypes
import numpy as np
from jax import lax
from jax.experimental import pallas as pl
from jax.experimental.pallas import tpu as pltpu
from jax.sharding import PartitionSpec as P

NX = 240
NY = 240
NZ = 240
PAD = 256
HALF_X = NX // 2
SLOTS = 8
HIGHEST = lax.Precision.HIGHEST
HIGH = lax.Precision.HIGH


def cos_sin(length):
    indices = np.arange(length)
    angles = (indices[:, None] * indices[None, :] % length) * (2.0 * math.pi / length)
    factor = 1.0 / math.sqrt(length)
    return np.cos(angles) * factor, np.sin(angles) * factor


def split_table():
    cos_part, sin_part = cos_sin(NY)
    table = np.zeros((PAD, 2 * PAD), np.float32)
    table[:NY, :NY] = cos_part
    table[:NY, PAD : PAD + NY] = sin_part
    high = table.astype(ml_dtypes.bfloat16)
    low = (table - high.astype(np.float32)).astype(ml_dtypes.bfloat16)
    return high, low


def halves(values):
    high = values.astype(jnp.bfloat16)
    low = (values - high.astype(jnp.float32)).astype(jnp.bfloat16)
    return high, low


def dot(a, b):
    return jnp.dot(a, b, preferred_element_type=jnp.float32)


def grid_kernel(
    source_ref, row_ref, half_ref, sticks_ref, potential_ref, y_ref, x_ref, out_ref,
    columns, waves, staged,
):
    rows = sticks_ref.shape[0]
    stick_count = source_ref.shape[0]
    lane_half = lax.broadcasted_iota(jnp.int32, (1, 128), 1) // 64
    lanes = waves.shape[1] // PAD
    parts = lanes // 2

    def clear(i, carry):
        columns[pl.ds(pl.multiple_of(i * PAD, PAD), PAD), :] = jnp.zeros((PAD, 128), jnp.float32)
        return carry

    lax.fori_loop(0, HALF_X, clear, 0)
    staged[:rows, :] = sticks_ref[...]
    staged[rows:, :] = pltpu.roll(sticks_ref[...], 64, 1)

    def scatter(g, carry):
        value = staged[pl.ds(source_ref[g], 1), :]
        pltpu.store(columns.at[pl.ds(row_ref[g], 1), :], value, mask=lane_half == half_ref[g])
        return carry

    lax.fori_loop(0, stick_count, scatter, 0, unroll=8)
    waves[:, NX * lanes :, :] = jnp.zeros((2, (PAD - NX) * lanes, 128), jnp.float32)

    def load(at):
        return jnp.concatenate([waves[0, at, :], waves[1, at, :]], axis=1)

    def store(at, values):
        waves[0, at, :] = values[:, :128]
        waves[1, at, :] = values[:, 128:]

    def times_y(values):
        high, low = halves(values)
        total = dot(high, y_ref[0]) + dot(high, y_ref[1]) + dot(low, y_ref[0])
        return total.reshape(2, 2, parts, 2 * PAD)

    def forward_y(i, carry):
        block = columns[pl.ds(pl.multiple_of(i * PAD, PAD), PAD), :]
        total = times_y(block.T)
        real = total[:, 0, :, :PAD] - total[:, 1, :, PAD:]
        imag = total[:, 0, :, PAD:] + total[:, 1, :, :PAD]
        both = jnp.stack([real, imag], axis=1).reshape(128, PAD)
        store(pl.ds(pl.multiple_of(i * 128, 128), 128), both)
        return carry

    lax.fori_loop(0, HALF_X, forward_y, 0)

    def times_x(values):
        high, low = halves(values)
        total = dot(x_ref[0], high) + dot(x_ref[1], high) + dot(x_ref[0], low)
        return total[:PAD], total[PAD:]

    def planes(q, carry):
        at_real = pl.ds(q, PAD, stride=lanes)
        at_imag = pl.ds(q + parts, PAD, stride=lanes)
        cos_real, sin_real = times_x(load(at_real))
        cos_imag, sin_imag = times_x(load(at_imag))
        local = potential_ref[lax.rem(q, SLOTS)]
        real = (cos_real - sin_imag) * local
        imag = (sin_real + cos_imag) * local
        cos_real, sin_real = times_x(real)
        cos_imag, sin_imag = times_x(imag)
        store(at_real, cos_real + sin_imag)
        store(at_imag, cos_imag - sin_real)
        return carry

    lax.fori_loop(0, parts, planes, 0)

    def backward_y(i, carry):
        total = times_y(load(pl.ds(pl.multiple_of(i * 128, 128), 128)))
        real = total[:, 0, :, :PAD] + total[:, 1, :, PAD:]
        imag = total[:, 1, :, :PAD] - total[:, 0, :, PAD:]
        both = jnp.stack([real, imag], axis=1).reshape(128, PAD)
        columns[pl.ds(pl.multiple_of(i * PAD, PAD), PAD), :] = both.T
        return carry

    lax.fori_loop(0, HALF_X, backward_y, 0)
    staged[...] = jnp.zeros_like(staged)

    def gather(g, carry):
        value = columns[pl.ds(row_ref[g], 1), :]
        pltpu.store(staged.at[pl.ds(source_ref[g], 1), :], value, mask=lane_half == half_ref[g])
        return carry

    lax.fori_loop(0, stick_count, gather, 0, unroll=8)
    out_ref[...] = staged[:rows, :] + pltpu.roll(staged[rows:, :], 64, 1)


def on_grid(source, row, half, sticks, potential):
    rows = sticks.shape[0]
    high, low = split_table()
    y_table = jnp.asarray(np.stack([high, low]))
    x_table = jnp.asarray(np.stack([high.T, low.T]))
    smem = pl.BlockSpec(memory_space=pltpu.SMEM)
    vmem = pl.BlockSpec(memory_space=pltpu.VMEM)
    return pl.pallas_call(
        grid_kernel,
        out_shape=jax.ShapeDtypeStruct((rows, 128), jnp.float32),
        in_specs=[smem] * 3 + [vmem] * 4,
        out_specs=vmem,
        scratch_shapes=[
            pltpu.VMEM((HALF_X * PAD, 128), jnp.float32),
            pltpu.VMEM((2, PAD * 64, 128), jnp.float32),
            pltpu.VMEM((2 * rows, 128), jnp.float32),
        ],
        compiler_params=pltpu.CompilerParams(vmem_limit_bytes=60 * 2**20),
    )(source, row, half, sticks, potential, y_table, x_table)


def per_device(coeffs, stick_count, stick_column, plane_owner, potential):
    tg_size = lax.axis_size("tg")
    fft_size = lax.axis_size("fft")
    devices = tg_size * fft_size
    bands, _, _, slot_count = coeffs.shape
    plane_slots = potential.shape[0]
    pairs = slot_count // 2
    chunk = -(-plane_slots // tg_size)
    tg = lax.axis_index("tg")
    device = tg * fft_size + lax.axis_index("fft")

    slot = jnp.arange(slot_count, dtype=jnp.int32)
    live = (slot[None, :] < stick_count[:, None]).reshape(-1)
    x = stick_column // NY
    half = x % 2
    row = jnp.where(live, x // 2 * PAD + stick_column % NY, NY)
    glob = jnp.arange(devices * slot_count, dtype=jnp.int32)
    within = glob % slot_count
    source = glob // slot_count * pairs + within % pairs
    source = source + jnp.where(within // pairs != half, devices * pairs, 0)

    planes = jnp.arange(NZ, dtype=jnp.int32)
    same_owner = plane_owner[None, :] == plane_owner[:, None]
    earlier = planes[None, :] < planes[:, None]
    ranks = jnp.sum((same_owner & earlier).astype(jnp.int32), axis=1)
    group = ranks // chunk
    place = ranks - jnp.minimum(group * chunk, plane_slots - SLOTS)
    plane_rows = (group * fft_size + plane_owner) * SLOTS + place
    table_rows = jnp.arange(devices * SLOTS, dtype=jnp.int32)
    pick = (table_rows[:, None] == plane_rows[None, :]).astype(jnp.float32)
    cos_part, sin_part = cos_sin(NZ)
    tables = jnp.asarray(np.concatenate([cos_part, sin_part], axis=1).astype(np.float32))
    lift = jnp.dot(pick, tables, precision=HIGHEST).reshape(devices, SLOTS, 2, NZ)
    lift_cos, lift_sin = lift[:, :, 0], lift[:, :, 1]
    forward = jnp.stack([jnp.stack([lift_cos, lift_sin]), jnp.stack([-lift_sin, lift_cos])])
    backward = jnp.stack([jnp.stack([lift_cos, -lift_sin]), jnp.stack([lift_sin, lift_cos])])

    start = jnp.minimum(tg * chunk, plane_slots - SLOTS)
    local = lax.dynamic_slice(potential, (start, 0), (SLOTS, NX * NY)).reshape(SLOTS, NX, NY)
    local = jnp.pad(local, ((0, 0), (0, PAD - NX), (0, PAD - NY)))

    lifted = jnp.einsum(
        "bczhj,cdmpz->mjhdbp", coeffs.reshape(bands, 2, NZ, 2, pairs), forward, precision=HIGH
    ).reshape(devices, pairs, 128)
    received = lax.all_to_all(lifted, ("tg", "fft"), split_axis=0, concat_axis=0, tiled=True)
    worked = on_grid(source, row, half, received.reshape(devices * pairs, 128), local)
    returned = lax.all_to_all(
        worked.reshape(devices, pairs, 128), ("tg", "fft"), split_axis=0, concat_axis=0, tiled=True
    )
    applied = jnp.einsum(
        "mjhcbp,cdmpz->bdzhj",
        returned.reshape(devices, pairs, 2, 2, bands, SLOTS), backward, precision=HIGH,
    ).reshape(bands, 2, NZ, slot_count)
    return jnp.where(slot < stick_count[device], applied, 0.0)


def solution(mesh):
    in_specs = (P(None, None, None, ("tg", "fft")), P(), P(), P(), P("fft", None))
    out_specs = P(None, None, None, ("tg", "fft"))
    return jax.shard_map(
        per_device, mesh=mesh, in_specs=in_specs, out_specs=out_specs, check_vma=False
    )
```

```python
import functools
import math

import jax
import jax.numpy as jnp
import ml_dtypes
import numpy as np
from jax import lax
from jax.experimental import pallas as pl
from jax.experimental.pallas import tpu as pltpu
from jax.sharding import PartitionSpec as P

NX = 240
NY = 240
NZ = 240
PAD = 256
FOLD = 128
LANES = 64
STRIDE = 72
BLOCKS = 121
UNROLL_Y = 11
UNROLL_X = 4
SLOTS = 8
HIGHEST = lax.Precision.HIGHEST
HIGH = lax.Precision.HIGH


def cos_sin(length):
    indices = np.arange(length)
    angles = (indices[:, None] * indices[None, :] % length) * (2.0 * math.pi / length)
    factor = 1.0 / math.sqrt(length)
    return np.cos(angles) * factor, np.sin(angles) * factor


def folded_table():
    cos_part, sin_part = cos_sin(NY)
    table = np.zeros((PAD, PAD), np.float32)
    table[: NY // 2 + 1, :NY] = cos_part[: NY // 2 + 1]
    table[FOLD : FOLD + NY // 2 + 1, :NY] = -sin_part[: NY // 2 + 1]
    high = table.astype(ml_dtypes.bfloat16)
    low = (table - high.astype(np.float32)).astype(ml_dtypes.bfloat16)
    return high, low


def mirrored(index):
    return jnp.where(index <= NY // 2, index, FOLD + NY - index)


def halves(values):
    high = values.astype(jnp.bfloat16)
    low = (values - high.astype(jnp.float32)).astype(jnp.bfloat16)
    return high, low


def dot(a, b):
    return jnp.dot(a, b, preferred_element_type=jnp.float32)


def grid_kernel(
    source_ref, row_ref, half_ref, sticks_ref, potential_ref, table_ref, turned_ref, out_ref,
    columns, waves, staged,
):
    rows = sticks_ref.shape[0]
    stick_count = source_ref.shape[0]
    lane_half = lax.broadcasted_iota(jnp.int32, (1, 128), 1) // 64
    parts = LANES // 2

    def clear(i, carry):
        columns[pl.ds(pl.multiple_of(i * PAD, PAD), PAD), :] = jnp.zeros((PAD, 128), jnp.float32)
        return carry

    lax.fori_loop(0, PAD // 2, clear, 0)
    staged[:rows, :] = sticks_ref[...]
    staged[rows:, :] = pltpu.roll(sticks_ref[...], 64, 1)

    def scatter(g, carry):
        value = staged[pl.ds(source_ref[g], 1), :]
        pltpu.store(columns.at[pl.ds(row_ref[g], 1), :], value, mask=lane_half == half_ref[g])
        return carry

    lax.fori_loop(0, stick_count, scatter, 0, unroll=8)
    for first, last in ((122, 128), (248, 256)):
        waves[:, first * STRIDE : last * STRIDE, :] = jnp.zeros((2, (last - first) * STRIDE, 128), jnp.float32)

    def load(at):
        return jnp.concatenate([waves[0, at, :], waves[1, at, :]], axis=1)

    def store(at, values):
        waves[0, at, :] = values[:, :128]
        waves[1, at, :] = values[:, 128:]

    def swapped(values):
        grid = values.reshape(2, 2, parts, FOLD)
        return grid[:, 0], grid[:, 1]

    def joined(real, imag):
        return jnp.stack([real, imag], axis=1).reshape(128, FOLD)

    def block_of(i):
        return i + jnp.where(i > 60, 3, 0)

    def forward_y(i, carry):
        block = block_of(i)
        base = pl.multiple_of(block * PAD, PAD)
        low_half = columns[pl.ds(base, FOLD), :]
        high_half = columns[pl.ds(base + FOLD, FOLD), :]
        even = (low_half + high_half).T
        odd_real, odd_imag = swapped((low_half - high_half).T)
        values = jnp.concatenate([even, joined(odd_imag, -odd_real)], axis=1)
        high, low = halves(values)
        total = dot(high, table_ref[0]) + dot(high, table_ref[1]) + dot(low, table_ref[0])
        for h in range(2):
            at = pl.ds(pl.multiple_of((block * 2 + h) * STRIDE, 8), LANES)
            store(at, total[h * LANES : (h + 1) * LANES])
        return carry

    lax.fori_loop(0, BLOCKS, forward_y, 0, unroll=UNROLL_Y)

    def three(table, values):
        high, low = halves(values)
        return dot(table[0], high) + dot(table[1], high) + dot(table[0], low)

    def planes(q, carry):
        at_real = pl.ds(q, PAD, stride=STRIDE)
        at_imag = pl.ds(q + parts, PAD, stride=STRIDE)
        real, imag = load(at_real), load(at_imag)
        for_real = jnp.concatenate([real[:FOLD] + real[FOLD:], imag[:FOLD] - imag[FOLD:]])
        for_imag = jnp.concatenate([imag[:FOLD] + imag[FOLD:], real[FOLD:] - real[:FOLD]])
        local = potential_ref[lax.rem(q, SLOTS)]
        real = three(table=turned_ref, values=for_real) * local
        imag = three(table=turned_ref, values=for_imag) * local
        real = three(table_ref, real)
        imag = three(table_ref, imag)
        store(at_real, jnp.concatenate([real[:FOLD] - imag[FOLD:], real[:FOLD] + imag[FOLD:]]))
        store(at_imag, jnp.concatenate([imag[:FOLD] + real[FOLD:], imag[:FOLD] - real[FOLD:]]))
        return carry

    lax.fori_loop(0, parts, planes, 0, unroll=UNROLL_X)

    def backward_y(i, carry):
        block = block_of(i)
        values = jnp.concatenate(
            [load(pl.ds(pl.multiple_of((block * 2 + h) * STRIDE, 8), LANES)) for h in range(2)]
        )
        high, low = halves(values)
        total = dot(high, turned_ref[0]) + dot(high, turned_ref[1]) + dot(low, turned_ref[0])
        cosine = total[:, :FOLD]
        sine_real, sine_imag = swapped(total[:, FOLD:])
        sine = joined(sine_imag, -sine_real)
        base = pl.multiple_of(block * PAD, PAD)
        columns[pl.ds(base, FOLD), :] = (cosine - sine).T
        columns[pl.ds(base + FOLD, FOLD), :] = (cosine + sine).T
        return carry

    lax.fori_loop(0, BLOCKS, backward_y, 0, unroll=UNROLL_Y)
    staged[...] = jnp.zeros_like(staged)

    def gather(g, carry):
        value = columns[pl.ds(row_ref[g], 1), :]
        pltpu.store(staged.at[pl.ds(source_ref[g], 1), :], value, mask=lane_half == half_ref[g])
        return carry

    lax.fori_loop(0, stick_count, gather, 0, unroll=8)
    out_ref[...] = staged[:rows, :] + pltpu.roll(staged[rows:, :], 64, 1)


def on_grid(source, row, half, sticks, potential):
    rows = sticks.shape[0]
    high, low = folded_table()
    table = jnp.asarray(np.stack([high, low]))
    turned = jnp.asarray(np.stack([high.T, low.T]))
    smem = pl.BlockSpec(memory_space=pltpu.SMEM)
    vmem = pl.BlockSpec(memory_space=pltpu.VMEM)
    return pl.pallas_call(
        grid_kernel,
        out_shape=jax.ShapeDtypeStruct((rows, 128), jnp.float32),
        in_specs=[smem] * 3 + [vmem] * 4,
        out_specs=vmem,
        scratch_shapes=[
            pltpu.VMEM((PAD // 2 * PAD, 128), jnp.float32),
            pltpu.VMEM((2, PAD * STRIDE, 128), jnp.float32),
            pltpu.VMEM((2 * rows, 128), jnp.float32),
        ],
        compiler_params=pltpu.CompilerParams(vmem_limit_bytes=60 * 2**20),
    )(source, row, half, sticks, potential, table, turned)


def per_device(coeffs, stick_count, stick_column, plane_owner, potential):
    tg_size = lax.axis_size("tg")
    fft_size = lax.axis_size("fft")
    devices = tg_size * fft_size
    bands, _, _, slot_count = coeffs.shape
    plane_slots = potential.shape[0]
    pairs = slot_count // 2
    chunk = -(-plane_slots // tg_size)
    tg = lax.axis_index("tg")
    device = tg * fft_size + lax.axis_index("fft")

    slot = jnp.arange(slot_count, dtype=jnp.int32)
    live = (slot[None, :] < stick_count[:, None]).reshape(-1)
    x = mirrored(stick_column // NY)
    half = x % 2
    row = jnp.where(live, x // 2 * PAD + mirrored(stick_column % NY), NY // 2 + 1)
    glob = jnp.arange(devices * slot_count, dtype=jnp.int32)
    within = glob % slot_count
    source = glob // slot_count * pairs + within % pairs
    source = source + jnp.where(within // pairs != half, devices * pairs, 0)

    planes = jnp.arange(NZ, dtype=jnp.int32)
    same_owner = plane_owner[None, :] == plane_owner[:, None]
    earlier = planes[None, :] < planes[:, None]
    ranks = jnp.sum((same_owner & earlier).astype(jnp.int32), axis=1)
    group = ranks // chunk
    place = ranks - jnp.minimum(group * chunk, plane_slots - SLOTS)
    plane_rows = (group * fft_size + plane_owner) * SLOTS + place
    table_rows = jnp.arange(devices * SLOTS, dtype=jnp.int32)
    pick = (table_rows[:, None] == plane_rows[None, :]).astype(jnp.float32)
    cos_part, sin_part = cos_sin(NZ)
    tables = jnp.asarray(np.concatenate([cos_part, sin_part], axis=1).astype(np.float32))
    lift = jnp.dot(pick, tables, precision=HIGHEST).reshape(devices, SLOTS, 2, NZ)
    lift_cos, lift_sin = lift[:, :, 0], lift[:, :, 1]
    forward = jnp.stack([jnp.stack([lift_cos, lift_sin]), jnp.stack([-lift_sin, lift_cos])])
    backward = jnp.stack([jnp.stack([lift_cos, -lift_sin]), jnp.stack([lift_sin, lift_cos])])

    start = jnp.minimum(tg * chunk, plane_slots - SLOTS)
    local = lax.dynamic_slice(potential, (start, 0), (SLOTS, NX * NY)).reshape(SLOTS, NX, NY)
    local = jnp.pad(local, ((0, 0), (0, PAD - NX), (0, PAD - NY)))

    lifted = jnp.einsum(
        "bczhj,cdmpz->mjhdbp", coeffs.reshape(bands, 2, NZ, 2, pairs), forward, precision=HIGH
    ).reshape(devices, pairs, 128)
    received = lax.all_to_all(lifted, ("tg", "fft"), split_axis=0, concat_axis=0, tiled=True)
    worked = on_grid(source, row, half, received.reshape(devices * pairs, 128), local)
    returned = lax.all_to_all(
        worked.reshape(devices, pairs, 128), ("tg", "fft"), split_axis=0, concat_axis=0, tiled=True
    )
    applied = jnp.einsum(
        "mjhcbp,cdmpz->bdzhj",
        returned.reshape(devices, pairs, 2, 2, bands, SLOTS), backward, precision=HIGH,
    ).reshape(bands, 2, NZ, slot_count)
    return jnp.where(slot < stick_count[device], applied, 0.0)


def solution(mesh):
    in_specs = (P(None, None, None, ("tg", "fft")), P(), P(), P(), P("fft", None))
    out_specs = P(None, None, None, ("tg", "fft"))
    return jax.shard_map(
        per_device, mesh=mesh, in_specs=in_specs, out_specs=out_specs, check_vma=False
    )
```

```python
import functools
import math

import jax
import jax.numpy as jnp
import ml_dtypes
import numpy as np
from jax import lax
from jax.experimental import pallas as pl
from jax.experimental.pallas import tpu as pltpu
from jax.sharding import PartitionSpec as P

NX = 240
NY = 240
NZ = 240
PAD = 256
FOLD = 128
LANES = 64
STRIDE = 72
BLOCKS = 121
UNROLL_Y = 11
UNROLL_G = 32
UNROLL_X = 8
SLOTS = 8
HIGHEST = lax.Precision.HIGHEST
HIGH = lax.Precision.HIGH


def cos_sin(length):
    indices = np.arange(length)
    angles = (indices[:, None] * indices[None, :] % length) * (2.0 * math.pi / length)
    factor = 1.0 / math.sqrt(length)
    return np.cos(angles) * factor, np.sin(angles) * factor


def folded_table():
    cos_part, sin_part = cos_sin(NY)
    table = np.zeros((PAD, PAD), np.float32)
    table[: NY // 2 + 1, :NY] = cos_part[: NY // 2 + 1]
    table[FOLD : FOLD + NY // 2 + 1, :NY] = -sin_part[: NY // 2 + 1]
    high = table.astype(ml_dtypes.bfloat16)
    low = (table - high.astype(np.float32)).astype(ml_dtypes.bfloat16)
    return high, low


def mirrored(index):
    return jnp.where(index <= NY // 2, index, FOLD + NY - index)


def halves(values):
    high = values.astype(jnp.bfloat16)
    low = (values - high.astype(jnp.float32)).astype(jnp.bfloat16)
    return high, low


def dot(a, b):
    return jnp.dot(a, b, preferred_element_type=jnp.float32)


def grid_kernel(
    source_ref, row_ref, half_ref, sticks_ref, potential_ref, table_ref, turned_ref, out_ref,
    columns, waves, staged,
):
    rows = sticks_ref.shape[0]
    stick_count = source_ref.shape[0]
    lane_half = lax.broadcasted_iota(jnp.int32, (1, 128), 1) // 64
    parts = LANES // 2

    def clear(i, carry):
        columns[pl.ds(pl.multiple_of(i * PAD, PAD), PAD), :] = jnp.zeros((PAD, 128), jnp.float32)
        return carry

    lax.fori_loop(0, PAD // 2, clear, 0)
    staged[:rows, :] = sticks_ref[...]
    staged[rows:, :] = pltpu.roll(sticks_ref[...], 64, 1)

    def scatter(g, carry):
        value = staged[pl.ds(source_ref[g], 1), :]
        pltpu.store(columns.at[pl.ds(row_ref[g], 1), :], value, mask=lane_half == half_ref[g])
        return carry

    lax.fori_loop(0, stick_count, scatter, 0, unroll=UNROLL_G)
    for first, last in ((122, 128), (248, 256)):
        waves[:, first * STRIDE : last * STRIDE, :] = jnp.zeros((2, (last - first) * STRIDE, 128), jnp.float32)

    def load(at):
        return jnp.concatenate([waves[0, at, :], waves[1, at, :]], axis=1)

    def store(at, values):
        waves[0, at, :] = values[:, :128]
        waves[1, at, :] = values[:, 128:]

    def swapped(values):
        grid = values.reshape(2, 2, parts, FOLD)
        return grid[:, 0], grid[:, 1]

    def joined(real, imag):
        return jnp.stack([real, imag], axis=1).reshape(128, FOLD)

    def block_of(i):
        return i + jnp.where(i > 60, 3, 0)

    def forward_y(i, carry):
        block = block_of(i)
        base = pl.multiple_of(block * PAD, PAD)
        low_half = columns[pl.ds(base, FOLD), :]
        high_half = columns[pl.ds(base + FOLD, FOLD), :]
        even = (low_half + high_half).T
        odd_real, odd_imag = swapped((low_half - high_half).T)
        values = jnp.concatenate([even, joined(odd_imag, -odd_real)], axis=1)
        high, low = halves(values)
        total = dot(high, table_ref[0]) + dot(high, table_ref[1]) + dot(low, table_ref[0])
        for h in range(2):
            at = pl.ds(pl.multiple_of((block * 2 + h) * STRIDE, 8), LANES)
            store(at, total[h * LANES : (h + 1) * LANES])
        return carry

    lax.fori_loop(0, BLOCKS, forward_y, 0, unroll=UNROLL_Y)

    def three(table, values):
        high, low = halves(values)
        return dot(table[0], high) + dot(table[1], high) + dot(table[0], low)

    def planes(q, carry):
        at_real = pl.ds(q, PAD, stride=STRIDE)
        at_imag = pl.ds(q + parts, PAD, stride=STRIDE)
        real, imag = load(at_real), load(at_imag)
        for_real = jnp.concatenate([real[:FOLD] + real[FOLD:], imag[:FOLD] - imag[FOLD:]])
        for_imag = jnp.concatenate([imag[:FOLD] + imag[FOLD:], real[FOLD:] - real[:FOLD]])
        local = potential_ref[lax.rem(q, SLOTS)]
        real = three(table=turned_ref, values=for_real) * local
        imag = three(table=turned_ref, values=for_imag) * local
        real = three(table_ref, real)
        imag = three(table_ref, imag)
        store(at_real, jnp.concatenate([real[:FOLD] - imag[FOLD:], real[:FOLD] + imag[FOLD:]]))
        store(at_imag, jnp.concatenate([imag[:FOLD] + real[FOLD:], imag[:FOLD] - real[FOLD:]]))
        return carry

    lax.fori_loop(0, parts, planes, 0, unroll=UNROLL_X)

    def backward_y(i, carry):
        block = block_of(i)
        values = jnp.concatenate(
            [load(pl.ds(pl.multiple_of((block * 2 + h) * STRIDE, 8), LANES)) for h in range(2)]
        )
        high, low = halves(values)
        total = dot(high, turned_ref[0]) + dot(high, turned_ref[1]) + dot(low, turned_ref[0])
        cosine = total[:, :FOLD]
        sine_real, sine_imag = swapped(total[:, FOLD:])
        sine = joined(sine_imag, -sine_real)
        base = pl.multiple_of(block * PAD, PAD)
        columns[pl.ds(base, FOLD), :] = (cosine - sine).T
        columns[pl.ds(base + FOLD, FOLD), :] = (cosine + sine).T
        return carry

    lax.fori_loop(0, BLOCKS, backward_y, 0, unroll=UNROLL_Y)
    staged[...] = jnp.zeros_like(staged)

    def gather(g, carry):
        value = columns[pl.ds(row_ref[g], 1), :]
        pltpu.store(staged.at[pl.ds(source_ref[g], 1), :], value, mask=lane_half == half_ref[g])
        return carry

    lax.fori_loop(0, stick_count, gather, 0, unroll=UNROLL_G)
    out_ref[...] = staged[:rows, :] + pltpu.roll(staged[rows:, :], 64, 1)


def on_grid(source, row, half, sticks, potential):
    rows = sticks.shape[0]
    high, low = folded_table()
    table = jnp.asarray(np.stack([high, low]))
    turned = jnp.asarray(np.stack([high.T, low.T]))
    smem = pl.BlockSpec(memory_space=pltpu.SMEM)
    vmem = pl.BlockSpec(memory_space=pltpu.VMEM)
    return pl.pallas_call(
        grid_kernel,
        out_shape=jax.ShapeDtypeStruct((rows, 128), jnp.float32),
        in_specs=[smem] * 3 + [vmem] * 4,
        out_specs=vmem,
        scratch_shapes=[
            pltpu.VMEM((PAD // 2 * PAD, 128), jnp.float32),
            pltpu.VMEM((2, PAD * STRIDE, 128), jnp.float32),
            pltpu.VMEM((2 * rows, 128), jnp.float32),
        ],
        compiler_params=pltpu.CompilerParams(vmem_limit_bytes=60 * 2**20),
    )(source, row, half, sticks, potential, table, turned)


def per_device(coeffs, stick_count, stick_column, plane_owner, potential):
    tg_size = lax.axis_size("tg")
    fft_size = lax.axis_size("fft")
    devices = tg_size * fft_size
    bands, _, _, slot_count = coeffs.shape
    plane_slots = potential.shape[0]
    pairs = slot_count // 2
    chunk = -(-plane_slots // tg_size)
    tg = lax.axis_index("tg")
    device = tg * fft_size + lax.axis_index("fft")

    slot = jnp.arange(slot_count, dtype=jnp.int32)
    live = (slot[None, :] < stick_count[:, None]).reshape(-1)
    x = mirrored(stick_column // NY)
    half = x % 2
    row = jnp.where(live, x // 2 * PAD + mirrored(stick_column % NY), NY // 2 + 1)
    glob = jnp.arange(devices * slot_count, dtype=jnp.int32)
    within = glob % slot_count
    source = glob // slot_count * pairs + within % pairs
    source = source + jnp.where(within // pairs != half, devices * pairs, 0)

    planes = jnp.arange(NZ, dtype=jnp.int32)
    same_owner = plane_owner[None, :] == plane_owner[:, None]
    earlier = planes[None, :] < planes[:, None]
    ranks = jnp.sum((same_owner & earlier).astype(jnp.int32), axis=1)
    group = ranks // chunk
    place = ranks - jnp.minimum(group * chunk, plane_slots - SLOTS)
    plane_rows = (group * fft_size + plane_owner) * SLOTS + place
    table_rows = jnp.arange(devices * SLOTS, dtype=jnp.int32)
    pick = (table_rows[:, None] == plane_rows[None, :]).astype(jnp.float32)
    cos_part, sin_part = cos_sin(NZ)
    tables = jnp.asarray(np.concatenate([cos_part, sin_part], axis=1).astype(np.float32))
    lift = jnp.dot(pick, tables, precision=HIGHEST).reshape(devices, SLOTS, 2, NZ)
    lift_cos, lift_sin = lift[:, :, 0], lift[:, :, 1]
    forward = jnp.stack([jnp.stack([lift_cos, lift_sin]), jnp.stack([-lift_sin, lift_cos])])
    backward = jnp.stack([jnp.stack([lift_cos, -lift_sin]), jnp.stack([lift_sin, lift_cos])])

    start = jnp.minimum(tg * chunk, plane_slots - SLOTS)
    local = lax.dynamic_slice(potential, (start, 0), (SLOTS, NX * NY)).reshape(SLOTS, NX, NY)
    local = jnp.pad(local, ((0, 0), (0, PAD - NX), (0, PAD - NY)))

    lifted = jnp.einsum(
        "bczhj,cdmpz->mjhdbp", coeffs.reshape(bands, 2, NZ, 2, pairs), forward, precision=HIGH
    ).reshape(devices, pairs, 128)
    received = lax.all_to_all(lifted, ("tg", "fft"), split_axis=0, concat_axis=0, tiled=True)
    worked = on_grid(source, row, half, received.reshape(devices * pairs, 128), local)
    returned = lax.all_to_all(
        worked.reshape(devices, pairs, 128), ("tg", "fft"), split_axis=0, concat_axis=0, tiled=True
    )
    applied = jnp.einsum(
        "mjhcbp,cdmpz->bdzhj",
        returned.reshape(devices, pairs, 2, 2, bands, SLOTS), backward, precision=HIGH,
    ).reshape(bands, 2, NZ, slot_count)
    return jnp.where(slot < stick_count[device], applied, 0.0)


def solution(mesh):
    in_specs = (P(None, None, None, ("tg", "fft")), P(), P(), P(), P("fft", None))
    out_specs = P(None, None, None, ("tg", "fft"))
    return jax.shard_map(
        per_device, mesh=mesh, in_specs=in_specs, out_specs=out_specs, check_vma=False
    )
```
